512 devices in a mesh: dom: 64 (over z, y), sub: 8 (over x, core).
Axes of the slice: x: 4, y: 4, z: 16, core: 2. Of those that a mesh axis runs over, the one named last changes fastest.
Arguments:
- fields: float32 [6, 56, 131072], P(None, None, ('dom', 'sub')), may hold values from -6 to 6
- metric: float32 [9, 131072], P(None, ('dom', 'sub')), may hold values from -4 to 4
- face_geom: float32 [4, 4, 131072], P(None, None, ('dom', 'sub')), as said below
- jacobian_ratio: float32 [56, 131072], P(None, ('dom', 'sub')), may hold values from 0.5 to 2
- curved: int32 [131072], P(('dom', 'sub')), may hold values 0 or 1
- derivatives: float32 [3, 56, 56], replicated, may hold values from -0.75 to 0.75
- lift_matrix: float32 [56, 84], replicated, may hold values from -0.625 to 0.625
- live_count: int32 [512], P(('dom', 'sub')), may hold values from 128 to 256, as said below
- send_list: int32 [512, 3, 8, 32], P(('dom', 'sub')), may hold values from 0 to 1023, as said below
- face_source: int32 [4, 131072], P(None, ('dom', 'sub')), may hold values from 0 to 1791, as said below
- face_permutation: int32 [4, 131072], P(None, ('dom', 'sub')), may hold values from 0 to 5
Outputs:
- advanced: float32 [6, 56, 131072], P(None, None, ('dom', 'sub'))
- section_register: float32 [6, 56, 131072], P(None, None, ('dom', 'sub'))
The draws below stay inside these ranges and needn't reach their ends.
Inputs may be any that keep to these rules, and one draw needn't show every extreme that they name: `live_count`: some device owns exactly 256 elements. `send_list`: each entry names a face f * 256 + e of an element that its device owns. `face_source`: an entry below 1024 names a face of an owned element of the same device; a larger entry names a ghost slot, never one whose source group lies outside the mesh. `face_geom`: unit normals and a positive surface scale.
All inputs are finite; a program needn't handle non-finite values. No bound on the sum of `curved` on one device may be relied on, other than what follows from the above.
Results may differ from the reference program's by a relative error of at most 0.0003.
Values sent between devices are 32-bit elements; how exact they have to be, the bound alone decides.
No kernel may reach another device: no remote copies, remote signals or barrier semaphores. Data moves between devices by JAX's collectives and lax.ppermute only.
A program may use at most 128 MiB of HBM per device.

```python
import math
import jax
import jax.numpy as jnp
import numpy as np
from jax import lax

NP = 56
NFP = 21
E_DEV = 256
CAP = 32
ELEMS = 131072
N_DOM = 64
N_SUB = 8


def live_counts(key):
    device_total = N_DOM * N_SUB
    count_key, full_key = jax.random.split(jax.random.fold_in(key, 11))
    counts = jax.random.randint(count_key, (device_total,), E_DEV // 2, E_DEV + 1)
    fullest = jax.random.randint(full_key, (), 0, device_total)
    return jnp.where(jnp.arange(device_total) == fullest, E_DEV, counts).astype(jnp.int32)


def peer_counts(key):
    device_total = N_DOM * N_SUB
    count_key, full_key = jax.random.split(jax.random.fold_in(key, 23))
    counts = jax.random.randint(count_key, (device_total, 3, N_SUB), CAP // 4, 3 * CAP // 4 + 1)
    target = jax.random.randint(full_key, (device_total,), 0, N_SUB)
    group_ids = jnp.arange(device_total, dtype=jnp.int32) // N_SUB
    chosen_offset = jnp.where(group_ids < N_DOM - 1, 2, 1)
    offsets = jnp.arange(3, dtype=jnp.int32)[None, :, None]
    sub_ids = jnp.arange(N_SUB, dtype=jnp.int32)[None, None, :]
    full_mask = (offsets == chosen_offset[:, None, None]) & (sub_ids == target[:, None, None])
    counts = jnp.where(full_mask, CAP, counts)
    edge_mask = (offsets == 0) & (group_ids[:, None, None] == 0) | (offsets == 2) & (group_ids[:, None, None] == N_DOM - 1)
    return jnp.where(edge_mask, 0, counts).astype(jnp.int32)


def draw_live_count(key, part):
    return live_counts(key)


def draw_send_list(key, part):
    device_total = N_DOM * N_SUB
    live_sizes = live_counts(key)
    face_key, elem_key = jax.random.split(jax.random.fold_in(key, 31))
    grid_shape = (device_total, 3, N_SUB, CAP)
    face_ids = jax.random.randint(face_key, grid_shape, 0, 4)
    elem_ids = jax.random.randint(elem_key, grid_shape, 0, live_sizes[:, None, None, None])
    return (face_ids * E_DEV + elem_ids).astype(jnp.int32)


def draw_face_source(key, part):
    device_total = N_DOM * N_SUB
    slot_total = 3 * N_SUB * CAP
    face_total = 4 * E_DEV
    live_sizes = live_counts(key)
    counts = peer_counts(key)
    device_ids = jnp.arange(device_total, dtype=jnp.int32)
    group_ids = device_ids // N_SUB
    own_sub = device_ids % N_SUB
    offsets = jnp.arange(3, dtype=jnp.int32)[None, :, None]
    sub_ids = jnp.arange(N_SUB, dtype=jnp.int32)[None, None, :]
    source_group = group_ids[:, None, None] - offsets + 1
    valid_mask = (source_group >= 0) & (source_group < N_DOM)
    sender = jnp.clip(source_group, 0, N_DOM - 1) * N_SUB + sub_ids
    incoming = counts[sender, offsets + 0 * sub_ids, own_sub[:, None, None] + 0 * sub_ids] * valid_mask
    slot_live = (jnp.arange(CAP, dtype=jnp.int32)[None, None, None, :] < incoming[..., None]).reshape(device_total, slot_total).astype(jnp.int32)
    slot_key, face_key, pick_face, pick_elem = jax.random.split(jax.random.fold_in(key, 47), 4)
    slot_perm = jax.vmap(lambda k: jax.random.permutation(k, slot_total))(jax.random.split(slot_key, device_total))
    slot_order = jnp.argsort((1 - slot_live) * slot_total + slot_perm, axis=1)
    live_slots = jnp.sum(slot_live, axis=1)
    face_elem = jnp.arange(face_total, dtype=jnp.int32) % E_DEV
    dead_face = (face_elem[None, :] >= live_sizes[:, None]).astype(jnp.int32)
    face_perm = jax.vmap(lambda k: jax.random.permutation(k, face_total))(jax.random.split(face_key, device_total))
    face_rank = jnp.argsort(jnp.argsort(dead_face * face_total + face_perm, axis=1), axis=1)
    remote = face_rank < live_slots[:, None]
    chosen = jnp.take_along_axis(slot_order, jnp.clip(face_rank, 0, slot_total - 1), axis=1)
    local_face = jax.random.randint(pick_face, (device_total, face_total), 0, 4) * E_DEV + jax.random.randint(pick_elem, (device_total, face_total), 0, live_sizes[:, None])
    source = jnp.where(remote, face_total + chosen, local_face)
    return jnp.transpose(source.reshape(device_total, 4, E_DEV), (1, 0, 2)).reshape(4, device_total * E_DEV).astype(jnp.int32)


def draw_face_geom(key, part):
    subkeys = jax.random.split(key, 3)
    grid_shape = (4, ELEMS)
    polar_angle = jnp.arccos(jax.random.uniform(subkeys[0], grid_shape, jnp.float32, -1.0, 1.0))
    azimuth = jax.random.uniform(subkeys[1], grid_shape, jnp.float32, -math.pi, math.pi)
    face_scale = jnp.exp(jax.random.uniform(subkeys[2], grid_shape, jnp.float32, 0.0, math.log(4.0)))
    return jnp.stack([jnp.sin(polar_angle) * jnp.cos(azimuth), jnp.sin(polar_angle) * jnp.sin(azimuth), jnp.cos(polar_angle), face_scale], axis=0).astype(jnp.float32)


def with_ends(values, stream_key, smallest, high):
    longest = values.shape.index(max(values.shape))
    spots = []
    for shift in (0, 1):
        where = [jax.random.randint(jax.random.fold_in(stream_key, axis), (), 0, length) for axis, length in enumerate(values.shape)]
        where[longest] = (where[longest] + shift) % values.shape[longest]
        spots.append(tuple(where))
    return values.at[spots[0]].set(smallest).at[spots[1]].set(high)


def shard_levels(own_key, shape, cuts, low, high):
    def one(axis_at, parts):
        draws = jax.random.uniform(jax.random.fold_in(jax.random.fold_in(own_key, 6), axis_at), (parts,), jnp.float32, low / len(cuts), high / len(cuts))
        return jnp.repeat(jnp.exp(draws), shape[axis_at] // parts).reshape((-1,) + (1,) * (len(shape) - axis_at - 1))

    loudness = one(*cuts[0])
    for cut in cuts[1:]:
        loudness = loudness * one(*cut)
    return loudness


def gaussian(rng, extent, deviation, most, cuts=(), held_as=jnp.bfloat16):
    gain = shard_levels(rng, extent, cuts, -0.22, 0.18) if cuts else 1.0
    entries = jax.random.normal(rng, extent, jnp.float32) * deviation * gain
    return jnp.minimum(jnp.maximum(entries, -most), most).astype(held_as)


def setup_inputs(seed: int = 0) -> dict:
    streams_of = jax.random.split(jax.random.key(seed), 12)
    return {
        "fields": gaussian(streams_of[0], (6, NP, ELEMS), 1.0, 6.0, ((2, 512),), jnp.float32),
        "metric": gaussian(streams_of[1], (9, ELEMS), 1.0, 4.0, ((1, 512),), jnp.float32),
        "face_geom": draw_face_geom(jax.random.fold_in(streams_of[11], 71), 0),
        "jacobian_ratio": jnp.clip(0.5 + 1.5 * jax.random.uniform(streams_of[3], (NP, ELEMS), jnp.float32) ** shard_levels(streams_of[3], (NP, ELEMS), ((1, 512),), -0.2, 0.2), 0.5, 2.0),
        "curved": with_ends((jax.random.randint(streams_of[4], (ELEMS,), 0, 4) < 1).astype(jnp.int32), jax.random.fold_in(streams_of[4], 1), 0, 1),
        "derivatives": gaussian(streams_of[5], (3, NP, NP), NP ** -0.5, 0.75, (), jnp.float32),
        "lift_matrix": gaussian(streams_of[6], (NP, 4 * NFP), (4 * NFP) ** -0.5, 0.625, (), jnp.float32),
        "live_count": draw_live_count(jax.random.fold_in(streams_of[11], 71), 0),
        "send_list": draw_send_list(jax.random.fold_in(streams_of[11], 71), 0),
        "face_source": draw_face_source(jax.random.fold_in(streams_of[11], 71), 0),
        "face_permutation": with_ends(jax.random.randint(streams_of[10], (4, ELEMS), 0, 6), jax.random.fold_in(streams_of[10], 1), 0, 5).astype(jnp.int32),
    }


RK_A = (0.0, -567301805773.0 / 1357537059087.0)
RK_B = (1432997174477.0 / 9575080441755.0, 5161836677717.0 / 13612068292357.0)
TIME_STEP = 0.5
SYMMETRIES = ((0, 1, 2), (1, 2, 0), (2, 0, 1), (0, 2, 1), (2, 1, 0), (1, 0, 2))


def node_tables():
    volume_nodes = [(i, j, k) for i in range(6) for j in range(6 - i) for k in range(6 - i - j)]
    volume_index = {v: n for n, v in enumerate(volume_nodes)}
    triangle = [(a, b) for a in range(6) for b in range(6 - a)]
    triangle_index = {t: n for n, t in enumerate(triangle)}
    face_nodes = np.array([[volume_index[(a, b, 0)] for a, b in triangle],
                           [volume_index[(a, 0, b)] for a, b in triangle],
                           [volume_index[(a, b, 5 - a - b)] for a, b in triangle],
                           [volume_index[(0, a, b)] for a, b in triangle]], np.int32)
    permuted = np.array([[triangle_index[((a, b, 5 - a - b)[q[0]], (a, b, 5 - a - b)[q[1]])] for a, b in triangle]
                         for q in SYMMETRIES], np.int32)
    return face_nodes, permuted


def volume_and_flux(current, exterior, interior, metric, face_geom, derivatives):
    slopes = jnp.einsum("mpq,cqe->mcpe", derivatives, current, precision=lax.Precision.HIGHEST)
    gradients = [metric[x] * slopes[0] + metric[3 + x] * slopes[1] + metric[6 + x] * slopes[2] for x in range(3)]
    diff_x, diff_y, diff_z = gradients
    volume = jnp.stack([
        -(diff_y[5] - diff_z[4]), -(diff_z[3] - diff_x[5]), -(diff_x[4] - diff_y[3]),
        diff_y[2] - diff_z[1], diff_z[0] - diff_x[2], diff_x[1] - diff_y[0]])
    jump = exterior - interior
    normal_x, normal_y, normal_z, face_scale = face_geom[0], face_geom[1], face_geom[2], face_geom[3]
    along_h = normal_x * jump[0] + normal_y * jump[1] + normal_z * jump[2]
    along_e = normal_x * jump[3] + normal_y * jump[4] + normal_z * jump[5]
    flux_all = jnp.stack([
        -(normal_y * jump[5] - normal_z * jump[4]) + jump[0] - along_h * normal_x,
        -(normal_z * jump[3] - normal_x * jump[5]) + jump[1] - along_h * normal_y,
        -(normal_x * jump[4] - normal_y * jump[3]) + jump[2] - along_h * normal_z,
        (normal_y * jump[2] - normal_z * jump[1]) + jump[3] - along_e * normal_x,
        (normal_z * jump[0] - normal_x * jump[2]) + jump[4] - along_e * normal_y,
        (normal_x * jump[1] - normal_y * jump[0]) + jump[5] - along_e * normal_z]) * (0.5 * face_scale)
    return volume, flux_all


def reference(fields, metric, face_geom, jacobian_ratio, curved, derivatives, lift_matrix, live_count, send_list, face_source, face_permutation):
    face_nodes, permuted = node_tables()
    node_table = jnp.asarray(face_nodes)
    turn_table = jnp.asarray(permuted)
    device_total = N_DOM * N_SUB
    local_ids = jnp.arange(E_DEV, dtype=jnp.int32)
    alive_all = (local_ids[None, :] < live_count[:, None]).astype(fields.dtype).reshape(-1)
    current = fields * alive_all
    residual = jnp.zeros_like(fields)
    offsets = jnp.arange(3, dtype=jnp.int32)[:, None, None]
    sub_ids = jnp.arange(N_SUB, dtype=jnp.int32)[None, :, None]
    lanes = jnp.arange(CAP, dtype=jnp.int32)[None, None, :]
    lift_three = lift_matrix.reshape(NP, 4, NFP)
    for step_index in range(2):
        def receive(device):
            group_id = device // N_SUB
            sub_id = device % N_SUB
            source_group = group_id - offsets + 1
            valid_mask = ((source_group >= 0) & (source_group < N_DOM)).astype(fields.dtype)
            sender = jnp.broadcast_to(jnp.clip(source_group, 0, N_DOM - 1) * N_SUB + sub_ids, (3, N_SUB, CAP))
            picked = send_list[sender, offsets + 0 * lanes, sub_id, lanes + 0 * sub_ids]
            face_id = picked // E_DEV
            elem_id = picked % E_DEV + sender * E_DEV
            node_index = node_table[face_id]
            values = current[:, node_index, elem_id[..., None]]
            values = values * valid_mask[None, :, :, :, None]
            return jnp.moveaxis(values, 4, 1).reshape(6, NFP, 3 * N_SUB * CAP)

        def evaluate(device):
            start = device * E_DEV
            block = lax.dynamic_slice_in_dim(current, start, E_DEV, 2)
            metric_block = lax.dynamic_slice_in_dim(metric, start, E_DEV, 1)
            geom_block = lax.dynamic_slice_in_dim(face_geom, start, E_DEV, 2)
            ratio_block = lax.dynamic_slice_in_dim(jacobian_ratio, start, E_DEV, 1)
            curved_block = lax.dynamic_slice_in_dim(curved, start, E_DEV, 0)
            source_block = lax.dynamic_slice_in_dim(face_source, start, E_DEV, 1)
            turn_block = lax.dynamic_slice_in_dim(face_permutation, start, E_DEV, 1)
            alive_block = lax.dynamic_slice_in_dim(alive_all, start, E_DEV, 0)
            interior = block[:, node_table.T, :]
            table = jnp.concatenate([interior.reshape(6, NFP, 4 * E_DEV), receive(device)], axis=2)
            gathered = jnp.take(table, source_block.reshape(-1), axis=2).reshape(6, NFP, 4, E_DEV)
            turn_index = jnp.transpose(turn_table[turn_block], (2, 0, 1))
            exterior = jnp.take_along_axis(gathered, turn_index[None], axis=1)
            volume, flux_all = volume_and_flux(block, exterior, interior, metric_block, geom_block, derivatives)
            lifted = jnp.einsum("nfi,cife->cne", lift_three, flux_all, precision=lax.Precision.HIGHEST)
            scaling = jnp.where(curved_block == 1, ratio_block, 1.0) * alive_block
            return (volume + lifted) * scaling

        rate = lax.map(evaluate, jnp.arange(device_total, dtype=jnp.int32))
        rate = jnp.transpose(rate, (1, 2, 0, 3)).reshape(6, NP, device_total * E_DEV)
        residual = RK_A[step_index] * residual + TIME_STEP * rate
        current = current + RK_B[step_index] * residual
    return current, residual
```

```python
import functools

import jax
import jax.numpy as jnp
import ml_dtypes
import numpy as np
from jax import lax
from jax.experimental import pallas as pl
from jax.experimental.pallas import tpu as pltpu
from jax.sharding import PartitionSpec as P

RK_A = (0.0, -567301805773.0 / 1357537059087.0)
RK_B = (1432997174477.0 / 9575080441755.0, 5161836677717.0 / 13612068292357.0)
TIME_STEP = 0.5
SYMMETRIES = ((0, 1, 2), (1, 2, 0), (2, 0, 1), (0, 2, 1), (2, 1, 0), (1, 0, 2))

NODES = 56
TRACE = 21
PADDED = 24
PACKED = 128
EXT = 6 * PADDED
F32 = jnp.float32
BF16 = jnp.bfloat16


def passed_along(array, axis, by):
    count = lax.axis_size(axis)
    pairs = [(i, i + by) for i in range(count) if 0 <= i + by < count]
    return lax.ppermute(array, axis, pairs)


def node_tables():
    volume_nodes = [(i, j, k) for i in range(6) for j in range(6 - i) for k in range(6 - i - j)]
    volume_index = {v: n for n, v in enumerate(volume_nodes)}
    triangle = [(a, b) for a in range(6) for b in range(6 - a)]
    triangle_index = {t: n for n, t in enumerate(triangle)}
    face_nodes = np.array(
        [
            [volume_index[a, b, 0] for a, b in triangle],
            [volume_index[a, 0, b] for a, b in triangle],
            [volume_index[a, b, 5 - a - b] for a, b in triangle],
            [volume_index[0, a, b] for a, b in triangle],
        ],
        np.int32,
    )
    permuted = np.array(
        [
            [triangle_index[(a, b, 5 - a - b)[q[0]], (a, b, 5 - a - b)[q[1]]] for a, b in triangle]
            for q in SYMMETRIES
        ],
        np.int32,
    )
    return (face_nodes, permuted)


def constant_matrices():
    face_nodes, permuted = node_tables()
    pick = np.zeros((4 * PACKED, 6 * NODES), np.float32)
    turn = np.zeros((6 * EXT, 2 * PACKED), np.float32)
    for c in range(6):
        for m in range(TRACE):
            for f in range(4):
                pick[f * PACKED + c * TRACE + m, c * NODES + face_nodes[f, m]] = 1
            for p in range(6):
                for part in range(2):
                    turn[p * EXT + c * PADDED + m, part * PACKED + c * TRACE + permuted[p, m]] = 1
    spread_lift = np.zeros((2, 4 * TRACE, 8 * PADDED), np.float32)
    for f in range(4):
        for m in range(TRACE):
            spread_lift[0, f * TRACE + m, f * PADDED + m] = 1
            spread_lift[0, f * TRACE + m, (4 + f) * PADDED + m] = 1
            spread_lift[1, f * TRACE + m, f * PADDED + m] = 1
    spread_node = np.zeros((2, NODES, 2 * NODES), np.float32)
    spread_node[0, :, :NODES] = spread_node[0, :, NODES:] = np.eye(NODES)
    spread_node[1, :, :NODES] = np.eye(NODES)
    return [a.astype(ml_dtypes.bfloat16) for a in (pick, turn, spread_lift, spread_node)]


def mm(a, b):
    return jnp.dot(a, b, preferred_element_type=F32)


def halves(x):
    high = x.astype(BF16)
    return high, (x - high.astype(F32)).astype(BF16)


def stacked_weights(weights, spread):
    high, low = halves(weights)
    return jnp.concatenate([mm(high, spread[0]), mm(low, spread[1])], axis=0).astype(BF16)


def stacked_values(x):
    high = x.astype(BF16).astype(F32)
    return jnp.concatenate([high, x - high], axis=0).astype(BF16)


def split_product(weights, values):
    both = mm(weights, values)
    rows = both.shape[0] // 2
    return both[:rows] + both[rows:]


def traces_of(state, pick):
    high, low = halves(state)
    parts = []
    for part in (high, low):
        all_faces = mm(pick, part).astype(BF16)
        parts.append(
            jnp.concatenate([all_faces[f * PACKED : (f + 1) * PACKED] for f in range(4)], axis=1)
        )
    return jnp.concatenate(parts, axis=0)


def pack(traces, send, out_ref):
    faces = traces.shape[1]
    slots = send.shape[1]
    columns = jnp.transpose(send, (1, 0))
    lane = lax.broadcasted_iota(jnp.int32, (slots, faces), 1)
    for j in range(8):
        rows = []
        for o in range(3):
            r = o * 8 + j
            hit = lane == columns[:, r : r + 1]
            rows.append(jnp.where(hit, 1.0, 0.0).astype(BF16))
        chosen = lax.dot_general(
            jnp.concatenate(rows, axis=0),
            traces,
            (((1,), (1,)), ((), ())),
            preferred_element_type=F32,
        )
        out_ref[j] = chosen[:, :PACKED] + chosen[:, PACKED:]


def one_hot(source, count, base):
    row = lax.broadcasted_iota(jnp.int32, (count, source.shape[1]), 0) + base
    return jnp.where(row == source, 1.0, 0.0).astype(BF16)


def turned(gathered, permutation, turn):
    variants = mm(turn, gathered)
    out = variants[:EXT]
    for p in range(1, 6):
        out = jnp.where(permutation == p, variants[p * EXT : (p + 1) * EXT], out)
    return out


def face_flux(jump, geom_ref, f):
    j = [jump[c * PADDED : (c + 1) * PADDED] for c in range(6)]
    nx, ny, nz, scale = (geom_ref[k, f : f + 1, :] for k in range(4))
    half = 0.5 * scale
    along_h = nx * j[0] + ny * j[1] + nz * j[2]
    along_e = nx * j[3] + ny * j[4] + nz * j[5]
    return [
        (-(ny * j[5] - nz * j[4]) + j[0] - along_h * nx) * half,
        (-(nz * j[3] - nx * j[5]) + j[1] - along_h * ny) * half,
        (-(nx * j[4] - ny * j[3]) + j[2] - along_h * nz) * half,
        (ny * j[2] - nz * j[1] + j[3] - along_e * nx) * half,
        (nz * j[0] - nx * j[2] + j[4] - along_e * ny) * half,
        (nx * j[1] - ny * j[0] + j[5] - along_e * nz) * half,
    ]


def lifted_from(fluxes, lift):
    out = []
    for c in range(6):
        x = jnp.concatenate([fluxes[f][c] for f in range(4)], axis=0)
        out.append(split_product(lift, stacked_values(x)))
    return out


def alive(live_ref, elements):
    return (lax.broadcasted_iota(jnp.int32, (1, elements), 1) < live_ref[0]).astype(F32)


def first_kernel(live_ref, fields_ref, send_ref, pick_ref, out_ref):
    elements = fields_ref.shape[2]
    state = fields_ref[...].reshape(6 * NODES, elements) * alive(live_ref, elements)
    pack(traces_of(state, pick_ref[...]), send_ref[...], out_ref)


def local_kernel(
    masked,
    live_ref,
    state_ref,
    metric_ref,
    geom_ref,
    source_ref,
    permutation_ref,
    derivatives_ref,
    lift_ref,
    pick_ref,
    turn_ref,
    spread_lift_ref,
    spread_node_ref,
    out_ref,
):
    elements = state_ref.shape[2]
    state = state_ref[...].reshape(6 * NODES, elements)
    if masked:
        state = state * alive(live_ref, elements)
    traces = traces_of(state, pick_ref[...])
    fluxes = []
    for f in range(4):
        gathered = mm(traces, one_hot(source_ref[f : f + 1, :], 4 * elements, 0)).astype(BF16)
        exterior = turned(gathered, permutation_ref[f : f + 1, :], turn_ref[...])
        interior = mm(turn_ref[:EXT], traces[:, f * elements : (f + 1) * elements])
        fluxes.append(face_flux(exterior - interior, geom_ref, f))
    lifted = lifted_from(fluxes, stacked_weights(lift_ref[...], spread_lift_ref))
    nabla = stacked_weights(derivatives_ref[...].reshape(3 * NODES, NODES), spread_node_ref)
    rate = lifted
    for c in range(6):
        slopes = split_product(nabla, stacked_values(state[c * NODES : (c + 1) * NODES]))
        s0, s1, s2 = (slopes[m * NODES : (m + 1) * NODES] for m in range(3))

        def gradient(x):
            return (
                metric_ref[x : x + 1] * s0
                + metric_ref[3 + x : 4 + x] * s1
                + metric_ref[6 + x : 7 + x] * s2
            )

        first, second = (c + 1) % 3, (c + 2) % 3
        base = 0 if c >= 3 else 3
        sign = -1.0 if c >= 3 else 1.0
        rate[base + first] = rate[base + first] + sign * gradient(second)
        rate[base + second] = rate[base + second] - sign * gradient(first)
    for c in range(6):
        out_ref[c] = rate[c]


def received_lift(ghost_refs, geom_ref, source_ref, permutation_ref, lift_ref, turn_ref, spread_ref):
    elements = source_ref.shape[1]
    columns = []
    for ref in ghost_refs:
        high, low = halves(jnp.transpose(ref, (1, 0)))
        columns.append(jnp.concatenate([high, low], axis=0))
    table = jnp.concatenate(columns, axis=1)
    fluxes = []
    for f in range(4):
        chosen = one_hot(source_ref[f : f + 1, :], table.shape[1], 4 * elements)
        gathered = mm(table, chosen).astype(BF16)
        exterior = turned(gathered, permutation_ref[f : f + 1, :], turn_ref[...])
        fluxes.append(face_flux(exterior, geom_ref, f))
    return lifted_from(fluxes, stacked_weights(lift_ref[...], spread_ref))


def final_kernel(
    step,
    live_ref,
    state_ref,
    residual_ref,
    partial_ref,
    down_ref,
    swapped_ref,
    up_ref,
    geom_ref,
    source_ref,
    permutation_ref,
    ratio_ref,
    curved_ref,
    lift_ref,
    turn_ref,
    spread_lift_ref,
    pick_ref,
    send_ref,
    *out_refs,
):
    elements = state_ref.shape[2]
    slots = swapped_ref.shape[1] // 3
    ghosts = [
        down_ref[...].reshape(-1, PACKED),
        swapped_ref[:, slots : 2 * slots].reshape(-1, PACKED),
        up_ref[...].reshape(-1, PACKED),
    ]
    lifted = received_lift(
        ghosts, geom_ref, source_ref, permutation_ref, lift_ref, turn_ref, spread_lift_ref
    )
    mask = alive(live_ref, elements)
    scaling = jnp.where(curved_ref[...] == 1, ratio_ref[...], 1.0) * mask
    state_out, residual_out = out_refs[:2]
    advanced = []
    for c in range(6):
        rate = (partial_ref[c] + lifted[c]) * scaling
        state = state_ref[c]
        if step == 0:
            state = state * mask
            residual = TIME_STEP * rate
        else:
            residual = RK_A[step] * residual_ref[c] + TIME_STEP * rate
        state = state + RK_B[step] * residual
        state_out[c] = state
        residual_out[c] = residual
        advanced.append(state)
    if step == 0:
        pack(
            traces_of(jnp.concatenate(advanced, axis=0), pick_ref[...]), send_ref[...], out_refs[2]
        )


VMEM = pl.BlockSpec(memory_space=pltpu.VMEM)
SMEM = pl.BlockSpec(memory_space=pltpu.SMEM)


def call(kernel, count, out_shape, name, flops):
    return pl.pallas_call(
        kernel,
        out_shape=out_shape,
        in_specs=[SMEM] + [VMEM] * count,
        out_specs=jax.tree.map(lambda _: VMEM, out_shape),
        compiler_params=pltpu.CompilerParams(vmem_limit_bytes=48 * 1024 * 1024),
        cost_estimate=pl.CostEstimate(flops=flops, bytes_accessed=4_000_000, transcendentals=0),
        name=name,
    )


def on_device(
    fields,
    metric,
    face_geom,
    jacobian_ratio,
    curved,
    derivatives,
    lift_matrix,
    live_count,
    send_list,
    face_source,
    face_permutation,
):
    elements = fields.shape[2]
    pick, turn, spread_lift, spread_node = (jnp.asarray(a) for a in constant_matrices())
    slots = send_list.shape[3]
    send = send_list.reshape(24, slots)
    curved_row = curved.reshape(1, elements)
    whole = jax.ShapeDtypeStruct((6, NODES, elements), F32)
    outgoing_shape = jax.ShapeDtypeStruct((8, 3 * slots, PACKED), F32)

    outgoing = call(first_kernel, 3, outgoing_shape, "first", 1_000_000_000)(
        live_count, fields, send, pick
    )
    current, residual = fields, fields
    for step in range(2):
        swapped = lax.all_to_all(outgoing, "sub", split_axis=0, concat_axis=0, tiled=True)
        partial = call(
            functools.partial(local_kernel, step == 0), 11, whole, "local", 3_000_000_000
        )(
            live_count,
            current,
            metric,
            face_geom,
            face_source,
            face_permutation,
            derivatives,
            lift_matrix,
            pick,
            turn,
            spread_lift,
            spread_node,
        )
        down = passed_along(swapped[:, :slots], "dom", -1)
        up = passed_along(swapped[:, 2 * slots :], "dom", 1)
        shapes = [whole, whole] + ([outgoing_shape] if step == 0 else [])
        current, residual, *rest = call(
            functools.partial(final_kernel, step), 16, shapes, "final", 3_000_000_000
        )(
            live_count,
            current,
            residual,
            partial,
            down,
            swapped,
            up,
            face_geom,
            face_source,
            face_permutation,
            jacobian_ratio,
            curved_row,
            lift_matrix,
            turn,
            spread_lift,
            pick,
            send,
        )
        if rest:
            outgoing = rest[0]
    return (current, residual)


def solution(mesh):
    return jax.shard_map(
        on_device,
        mesh=mesh,
        in_specs=(
            P(None, None, ("dom", "sub")),
            P(None, ("dom", "sub")),
            P(None, None, ("dom", "sub")),
            P(None, ("dom", "sub")),
            P(("dom", "sub")),
            P(),
            P(),
            P(("dom", "sub")),
            P(("dom", "sub"), None, None, None),
            P(None, ("dom", "sub")),
            P(None, ("dom", "sub")),
        ),
        out_specs=(P(None, None, ("dom", "sub")), P(None, None, ("dom", "sub"))),
        check_vma=False,
    )
```

```python
import functools

import jax
import jax.numpy as jnp
import ml_dtypes
import numpy as np
from jax import lax
from jax.experimental import pallas as pl
from jax.experimental.pallas import tpu as pltpu
from jax.sharding import PartitionSpec as P

RK_A = (0.0, -567301805773.0 / 1357537059087.0)
RK_B = (1432997174477.0 / 9575080441755.0, 5161836677717.0 / 13612068292357.0)
TIME_STEP = 0.5
SYMMETRIES = ((0, 1, 2), (1, 2, 0), (2, 0, 1), (0, 2, 1), (2, 1, 0), (1, 0, 2))

NODES = 56
TRACE = 21
PADDED = 24
PACKED = 128
EXT = 6 * PADDED
HALF = 3 * PADDED
F32 = jnp.float32
BF16 = jnp.bfloat16


def swapped_pairs(array, axis, first):
    count = lax.axis_size(axis)
    pairs = []
    for low in range(first, count - 1, 2):
        pairs += [(low, low + 1), (low + 1, low)]
    return lax.ppermute(array, axis, pairs)


def node_tables():
    volume_nodes = [(i, j, k) for i in range(6) for j in range(6 - i) for k in range(6 - i - j)]
    volume_index = {v: n for n, v in enumerate(volume_nodes)}
    triangle = [(a, b) for a in range(6) for b in range(6 - a)]
    triangle_index = {t: n for n, t in enumerate(triangle)}
    face_nodes = np.array(
        [
            [volume_index[a, b, 0] for a, b in triangle],
            [volume_index[a, 0, b] for a, b in triangle],
            [volume_index[a, b, 5 - a - b] for a, b in triangle],
            [volume_index[0, a, b] for a, b in triangle],
        ],
        np.int32,
    )
    permuted = np.array(
        [
            [triangle_index[(a, b, 5 - a - b)[q[0]], (a, b, 5 - a - b)[q[1]]] for a, b in triangle]
            for q in SYMMETRIES
        ],
        np.int32,
    )
    return (face_nodes, permuted)


def constant_matrices():
    face_nodes, permuted = node_tables()
    pick = np.zeros((4 * PACKED, 6 * NODES), np.float32)
    pad = np.zeros((EXT, 2 * PACKED), np.float32)
    turn = np.zeros((6 * HALF, 2 * HALF), np.float32)
    for m in range(TRACE):
        for c in range(6):
            for f in range(4):
                pick[f * PACKED + c * TRACE + m, c * NODES + face_nodes[f, m]] = 1
            for part in range(2):
                pad[c * PADDED + m, part * PACKED + c * TRACE + m] = 1
        for c in range(3):
            for p in range(6):
                for part in range(2):
                    turn[p * HALF + c * PADDED + m, part * HALF + c * PADDED + permuted[p, m]] = 1
    spread_lift = np.zeros((2, 4 * TRACE, 8 * PADDED), np.float32)
    for f in range(4):
        for m in range(TRACE):
            spread_lift[0, f * TRACE + m, f * PADDED + m] = 1
            spread_lift[0, f * TRACE + m, (4 + f) * PADDED + m] = 1
            spread_lift[1, f * TRACE + m, f * PADDED + m] = 1
    spread_node = np.zeros((2, NODES, 2 * NODES), np.float32)
    spread_node[0, :, :NODES] = spread_node[0, :, NODES:] = np.eye(NODES)
    spread_node[1, :, :NODES] = np.eye(NODES)
    return [a.astype(ml_dtypes.bfloat16) for a in (pick, pad, turn, spread_lift, spread_node)]


def mm(a, b):
    return jnp.dot(a, b, preferred_element_type=F32)


def halves(x):
    high = x.astype(BF16)
    return high, (x - high.astype(F32)).astype(BF16)


def stacked_weights(weights, spread):
    high, low = halves(weights)
    return jnp.concatenate([mm(high, spread[0]), mm(low, spread[1])], axis=0).astype(BF16)


def stacked_values(x):
    high = x.astype(BF16).astype(F32)
    return jnp.concatenate([high, x - high], axis=0).astype(BF16)


def split_product(weights, values):
    both = mm(weights, values)
    rows = both.shape[0] // 2
    return both[:rows] + both[rows:]


def traces_of(state, pick):
    high, low = halves(state)
    parts = []
    for part in (high, low):
        all_faces = mm(pick, part).astype(BF16)
        parts.append(
            jnp.concatenate([all_faces[f * PACKED : (f + 1) * PACKED] for f in range(4)], axis=1)
        )
    return jnp.concatenate(parts, axis=0)


def even_group():
    return lax.rem(lax.axis_index("dom"), 2) == 0


def outgoing_choice(send, faces):
    even = even_group()
    low, own, high = send[:8], send[8:16], send[16:]
    ordered = [jnp.where(even, high, low), own, jnp.where(even, low, high)]
    columns = jnp.transpose(jnp.concatenate(ordered, axis=0), (1, 0))
    lane = lax.broadcasted_iota(jnp.int32, (send.shape[1], faces), 1)
    rows = []
    for j in range(8):
        for block in range(3):
            r = block * 8 + j
            rows.append(jnp.where(lane == columns[:, r : r + 1], 1.0, 0.0).astype(BF16))
    return jnp.concatenate(rows, axis=0)


def pack(choice, traces, out_ref):
    chosen = lax.dot_general(
        choice, traces, (((1,), (1,)), ((), ())), preferred_element_type=F32
    )
    out_ref[...] = (chosen[:, :PACKED] + chosen[:, PACKED:]).reshape(out_ref.shape)


def one_hot(source, count, base):
    row = lax.broadcasted_iota(jnp.int32, (count, source.shape[1]), 0) + base
    return jnp.where(row == source, 1.0, 0.0).astype(BF16)


def row_of_faces(ref, lead=()):
    return jnp.concatenate([ref[lead + (slice(f, f + 1),)] for f in range(4)], axis=1)


def flux_h(traces, n, half):
    j = [traces[c * PADDED : (c + 1) * PADDED] for c in range(6)]
    along = n[0] * j[0] + n[1] * j[1] + n[2] * j[2]
    parts = [
        (-(n[1] * j[5] - n[2] * j[4]) + j[0] - along * n[0]) * half,
        (-(n[2] * j[3] - n[0] * j[5]) + j[1] - along * n[1]) * half,
        (-(n[0] * j[4] - n[1] * j[3]) + j[2] - along * n[2]) * half,
    ]
    return jnp.concatenate(parts, axis=0)


def turned(flux, permutation, turn):
    variants = mm(turn, stacked_values(flux))
    out = variants[:HALF]
    for p in range(1, 6):
        out = jnp.where(permutation == p, variants[p * HALF : (p + 1) * HALF], out)
    return out


def lifted_from(flux, n, lift):
    h = [flux[c * PADDED : (c + 1) * PADDED] for c in range(3)]
    e = [n[(c + 1) % 3] * h[(c + 2) % 3] - n[(c + 2) % 3] * h[(c + 1) % 3] for c in range(3)]
    elements = flux.shape[1] // 4
    out = []
    for x in h + e:
        x = jnp.concatenate([x[:, f * elements : (f + 1) * elements] for f in range(4)], axis=0)
        out.append(split_product(lift, stacked_values(x)))
    return out


def normals(geom_ref):
    n = [row_of_faces(geom_ref, (k,)) for k in range(4)]
    return n[:3], 0.5 * n[3]


def alive(live_ref, elements):
    return (lax.broadcasted_iota(jnp.int32, (1, elements), 1) < live_ref[0]).astype(F32)


def first_kernel(
    live_ref,
    fields_hbm,
    send_hbm,
    pick_hbm,
    out_ref,
    choice_ref,
    state_ref,
    traces_ref,
    fields_ref,
    send_ref,
    pick_ref,
    sems,
):
    elements = fields_ref.shape[2]
    send_copy = pltpu.make_async_copy(send_hbm, send_ref, sems.at[0])
    fields_copy = pltpu.make_async_copy(fields_hbm, fields_ref, sems.at[1])
    pick_copy = pltpu.make_async_copy(pick_hbm, pick_ref, sems.at[2])
    send_copy.start()
    fields_copy.start()
    pick_copy.start()
    send_copy.wait()
    choice_ref[...] = outgoing_choice(send_ref[...], 4 * elements)
    fields_copy.wait()
    state = fields_ref[...].reshape(6 * NODES, elements) * alive(live_ref, elements)
    state_ref[...] = state.reshape(state_ref.shape)
    pick_copy.wait()
    traces = traces_of(state, pick_ref[...])
    traces_ref[...] = traces
    pack(choice_ref[...], traces, out_ref)


def local_kernel(
    step,
    live_ref,
    state_ref,
    traces_ref,
    metric_ref,
    geom_ref,
    source_ref,
    permutation_ref,
    derivatives_ref,
    lift_ref,
    pad_ref,
    turn_ref,
    spread_lift_ref,
    spread_node_ref,
    ratio_ref,
    curved_ref,
    out_ref,
    *prepared,
):
    elements = state_ref.shape[2]
    n, half = normals(geom_ref)
    source, permutation = row_of_faces(source_ref), row_of_faces(permutation_ref)
    lift = stacked_weights(lift_ref[...], spread_lift_ref)
    traces = traces_ref[...]
    gathered = []
    for f in range(4):
        chosen = one_hot(source_ref[f : f + 1], 4 * elements, 0)
        gathered.append(mm(traces, chosen).astype(BF16))
    gathered = jnp.concatenate(gathered, axis=1)
    flux = turned(flux_h(mm(pad_ref[...], gathered), n, half), permutation, turn_ref[...])
    flux = flux - flux_h(mm(pad_ref[...], traces), n, half)
    rate = lifted_from(flux, n, lift)
    nabla = stacked_weights(derivatives_ref[...].reshape(3 * NODES, NODES), spread_node_ref)
    for c in range(6):
        slopes = split_product(nabla, stacked_values(state_ref[c]))
        s0, s1, s2 = (slopes[m * NODES : (m + 1) * NODES] for m in range(3))

        def gradient(x):
            return (
                metric_ref[x : x + 1] * s0
                + metric_ref[3 + x : 4 + x] * s1
                + metric_ref[6 + x : 7 + x] * s2
            )

        first, second = (c + 1) % 3, (c + 2) % 3
        base = 0 if c >= 3 else 3
        sign = -1.0 if c >= 3 else 1.0
        rate[base + first] = rate[base + first] + sign * gradient(second)
        rate[base + second] = rate[base + second] - sign * gradient(first)
    for c in range(6):
        out_ref[c] = rate[c]
    if step == 0:
        choice_ref, lift_out_ref, scaling_ref = prepared
        lift_out_ref[...] = lift
        ratio = jnp.where(curved_ref[...] == 1, ratio_ref[...], 1.0)
        scaling_ref[...] = ratio * alive(live_ref, elements)
        even = even_group()
        block = choice_ref.shape[0] // 2
        start = 4 * elements
        near, far = start, start + 2 * block
        first_base = jnp.where(even, near, far)
        other_base = jnp.where(even, far, near)
        choice_ref[:block] = one_hot(source, block, first_base)
        choice_ref[block:] = one_hot(source, block, other_base)


def received_flux(tables, choice, geom_ref, permutation_ref, pad_ref, turn_ref):
    columns = []
    for table in tables:
        high, low = halves(jnp.transpose(table, (1, 0)))
        columns.append(jnp.concatenate([high, low], axis=0))
    n, half = normals(geom_ref)
    gathered = mm(jnp.concatenate(columns, axis=1), choice).astype(BF16)
    flux = flux_h(mm(pad_ref[...], gathered), n, half)
    return turned(flux, row_of_faces(permutation_ref), turn_ref[...]), n


def own_kernel(
    live_ref,
    partial_ref,
    swapped_ref,
    geom_ref,
    source_ref,
    permutation_ref,
    lift_ref,
    pad_ref,
    turn_ref,
    out_ref,
):
    slots = swapped_ref.shape[1] // 3
    table = swapped_ref[:, slots : 2 * slots].reshape(-1, PACKED)
    count = table.shape[0]
    base = 4 * source_ref.shape[1] + count
    choice = one_hot(row_of_faces(source_ref), count, base)
    flux, n = received_flux([table], choice, geom_ref, permutation_ref, pad_ref, turn_ref)
    lifted = lifted_from(flux, n, lift_ref[...])
    for c in range(6):
        out_ref[c] = partial_ref[c] + lifted[c]


def final_kernel(
    step,
    live_ref,
    state_ref,
    residual_ref,
    partial_ref,
    first_ref,
    other_ref,
    choice_ref,
    geom_ref,
    permutation_ref,
    scaling_ref,
    lift_ref,
    pad_ref,
    turn_ref,
    pick_ref,
    outgoing_choice_ref,
    *out_refs,
):
    tables = [r[...].reshape(-1, PACKED) for r in (first_ref, other_ref)]
    flux, n = received_flux(
        tables, choice_ref[...], geom_ref, permutation_ref, pad_ref, turn_ref
    )
    lifted = lifted_from(flux, n, lift_ref[...])
    scaling = scaling_ref[...]
    state_out, residual_out = out_refs[:2]
    advanced = []
    for c in range(6):
        residual = TIME_STEP * ((partial_ref[c] + lifted[c]) * scaling)
        if step > 0:
            residual = RK_A[step] * residual_ref[c] + residual
        state = state_ref[c] + RK_B[step] * residual
        state_out[c] = state
        residual_out[c] = residual
        advanced.append(state)
    if step == 0:
        traces = traces_of(jnp.concatenate(advanced, axis=0), pick_ref[...])
        out_refs[3][...] = traces
        pack(outgoing_choice_ref[...], traces, out_refs[2])


VMEM = pl.BlockSpec(memory_space=pltpu.VMEM)
SMEM = pl.BlockSpec(memory_space=pltpu.SMEM)
HBM = pl.BlockSpec(memory_space=pltpu.HBM)


def call(kernel, space, count, out_shape, name, flops, scratch=()):
    return pl.pallas_call(
        kernel,
        out_shape=out_shape,
        in_specs=[SMEM] + [space] * count,
        out_specs=jax.tree.map(lambda _: VMEM, out_shape),
        scratch_shapes=scratch,
        compiler_params=pltpu.CompilerParams(vmem_limit_bytes=40 * 1024 * 1024),
        cost_estimate=pl.CostEstimate(flops=flops, bytes_accessed=4_000_000, transcendentals=0),
        name=name,
    )


def on_device(
    fields,
    metric,
    face_geom,
    jacobian_ratio,
    curved,
    derivatives,
    lift_matrix,
    live_count,
    send_list,
    face_source,
    face_permutation,
):
    elements = fields.shape[2]
    pick, pad, turn, spread_lift, spread_node = (jnp.asarray(a) for a in constant_matrices())
    slots = send_list.shape[3]
    send = send_list.reshape(24, slots)
    curved_row = curved.reshape(1, elements)
    shape = jax.ShapeDtypeStruct
    whole = shape((6, NODES, elements), F32)
    outgoing_shape = shape((8, 3 * slots, PACKED), F32)
    traces_shape = shape((2 * PACKED, 4 * elements), BF16)

    outgoing, outgoing_rows, current, traces = call(
        first_kernel,
        HBM,
        3,
        [outgoing_shape, shape((24 * slots, 4 * elements), BF16), whole, traces_shape],
        "first",
        1_000_000_000,
        scratch=[
            pltpu.VMEM(fields.shape, F32),
            pltpu.VMEM(send.shape, jnp.int32),
            pltpu.VMEM(pick.shape, BF16),
            pltpu.SemaphoreType.DMA((3,)),
        ],
    )(live_count, fields, send, pick)
    residual = current
    for step in range(2):
        swapped = lax.all_to_all(outgoing, "sub", split_axis=0, concat_axis=0, tiled=True)
        shapes = [whole]
        if step == 0:
            shapes += [
                shape((16 * slots, 4 * elements), BF16),
                shape((2 * NODES, 8 * PADDED), BF16),
                shape((NODES, elements), F32),
            ]
        partial, *prepared = call(
            functools.partial(local_kernel, step), VMEM, 14, shapes, "local", 4_000_000_000
        )(
            live_count,
            current,
            traces,
            metric,
            face_geom,
            face_source,
            face_permutation,
            derivatives,
            lift_matrix,
            pad,
            turn,
            spread_lift,
            spread_node,
            jacobian_ratio,
            curved_row,
        )
        if step == 0:
            choice, lift, scaling = prepared
        swapped, partial = lax.optimization_barrier((swapped, partial))
        first = swapped_pairs(swapped[:, :slots], "dom", 0)
        other = swapped_pairs(swapped[:, 2 * slots :], "dom", 1)
        partial = call(own_kernel, VMEM, 8, whole, "own", 1_500_000_000)(
            live_count,
            partial,
            swapped,
            face_geom,
            face_source,
            face_permutation,
            lift,
            pad,
            turn,
        )
        shapes = [whole, whole] + ([outgoing_shape, traces_shape] if step == 0 else [])
        current, residual, *rest = call(
            functools.partial(final_kernel, step), VMEM, 14, shapes, "final", 3_000_000_000
        )(
            live_count,
            current,
            residual,
            partial,
            first,
            other,
            choice,
            face_geom,
            face_permutation,
            scaling,
            lift,
            pad,
            turn,
            pick,
            outgoing_rows,
        )
        if rest:
            outgoing, traces = rest
    return (current, residual)


def solution(mesh):
    return jax.shard_map(
        on_device,
        mesh=mesh,
        in_specs=(
            P(None, None, ("dom", "sub")),
            P(None, ("dom", "sub")),
            P(None, None, ("dom", "sub")),
            P(None, ("dom", "sub")),
            P(("dom", "sub")),
            P(),
            P(),
            P(("dom", "sub")),
            P(("dom", "sub"), None, None, None),
            P(None, ("dom", "sub")),
            P(None, ("dom", "sub")),
        ),
        out_specs=(P(None, None, ("dom", "sub")), P(None, None, ("dom", "sub"))),
        check_vma=False,
    )
```

```python
import functools

import jax
import jax.numpy as jnp
import ml_dtypes
import numpy as np
from jax import lax
from jax.experimental import pallas as pl
from jax.experimental.pallas import tpu as pltpu
from jax.sharding import PartitionSpec as P

RK_A = (0.0, -567301805773.0 / 1357537059087.0)
RK_B = (1432997174477.0 / 9575080441755.0, 5161836677717.0 / 13612068292357.0)
TIME_STEP = 0.5
SYMMETRIES = ((0, 1, 2), (1, 2, 0), (2, 0, 1), (0, 2, 1), (2, 1, 0), (1, 0, 2))

NODES = 56
TRACE = 21
PADDED = 24
PACKED = 128
EXT = 6 * PADDED
HALF = 3 * PADDED
F32 = jnp.float32
BF16 = jnp.bfloat16


def swapped_pairs(array, axis, first):
    count = lax.axis_size(axis)
    pairs = []
    for low in range(first, count - 1, 2):
        pairs += [(low, low + 1), (low + 1, low)]
    return lax.ppermute(array, axis, pairs)


def node_tables():
    volume_nodes = [(i, j, k) for i in range(6) for j in range(6 - i) for k in range(6 - i - j)]
    volume_index = {v: n for n, v in enumerate(volume_nodes)}
    triangle = [(a, b) for a in range(6) for b in range(6 - a)]
    triangle_index = {t: n for n, t in enumerate(triangle)}
    face_nodes = np.array(
        [
            [volume_index[a, b, 0] for a, b in triangle],
            [volume_index[a, 0, b] for a, b in triangle],
            [volume_index[a, b, 5 - a - b] for a, b in triangle],
            [volume_index[0, a, b] for a, b in triangle],
        ],
        np.int32,
    )
    permuted = np.array(
        [
            [triangle_index[(a, b, 5 - a - b)[q[0]], (a, b, 5 - a - b)[q[1]]] for a, b in triangle]
            for q in SYMMETRIES
        ],
        np.int32,
    )
    return (face_nodes, permuted)


def constant_matrices():
    face_nodes, permuted = node_tables()
    pick = np.zeros((4 * PACKED, 6 * NODES), np.float32)
    pad = np.zeros((EXT, 2 * PACKED), np.float32)
    turn = np.zeros((6 * HALF, 2 * HALF), np.float32)
    for m in range(TRACE):
        for c in range(6):
            for f in range(4):
                pick[f * PACKED + c * TRACE + m, c * NODES + face_nodes[f, m]] = 1
            for part in range(2):
                pad[c * PADDED + m, part * PACKED + c * TRACE + m] = 1
        for c in range(3):
            for p in range(6):
                for part in range(2):
                    turn[p * HALF + c * PADDED + m, part * HALF + c * PADDED + permuted[p, m]] = 1
    spread_lift = np.zeros((2, 4 * TRACE, 8 * PADDED), np.float32)
    for f in range(4):
        for m in range(TRACE):
            spread_lift[0, f * TRACE + m, f * PADDED + m] = 1
            spread_lift[0, f * TRACE + m, (4 + f) * PADDED + m] = 1
            spread_lift[1, f * TRACE + m, f * PADDED + m] = 1
    spread_node = np.zeros((2, NODES, 2 * NODES), np.float32)
    spread_node[0, :, :NODES] = spread_node[0, :, NODES:] = np.eye(NODES)
    spread_node[1, :, :NODES] = np.eye(NODES)
    return [a.astype(ml_dtypes.bfloat16) for a in (pick, pad, turn, spread_lift, spread_node)]


def mm(a, b):
    return jnp.dot(a, b, preferred_element_type=F32)


def halves(x):
    high = x.astype(BF16)
    return high, (x - high.astype(F32)).astype(BF16)


def stacked_weights(weights, spread):
    high, low = halves(weights)
    return jnp.concatenate([mm(high, spread[0]), mm(low, spread[1])], axis=0).astype(BF16)


def stacked_values(x):
    high = x.astype(BF16).astype(F32)
    return jnp.concatenate([high, x - high], axis=0).astype(BF16)


def split_product(weights, values):
    both = mm(weights, values)
    rows = both.shape[0] // 2
    return both[:rows] + both[rows:]


def traces_of(state, pick):
    high, low = halves(state)
    parts = []
    for part in (high, low):
        all_faces = mm(pick, part).astype(BF16)
        parts.append(
            jnp.concatenate([all_faces[f * PACKED : (f + 1) * PACKED] for f in range(4)], axis=1)
        )
    return jnp.concatenate(parts, axis=0)


def even_group():
    return lax.rem(lax.axis_index("dom"), 2) == 0


def outgoing_choice(send, faces):
    even = even_group()
    low, own, high = send[:8], send[8:16], send[16:]
    ordered = [jnp.where(even, high, low), own, jnp.where(even, low, high)]
    columns = jnp.transpose(jnp.concatenate(ordered, axis=0), (1, 0))
    lane = lax.broadcasted_iota(jnp.int32, (send.shape[1], faces), 1)
    rows = []
    for j in range(8):
        for block in range(3):
            r = block * 8 + j
            rows.append(jnp.where(lane == columns[:, r : r + 1], 1.0, 0.0).astype(BF16))
    return jnp.concatenate(rows, axis=0)


def pack(choice, traces, out_ref):
    chosen = lax.dot_general(
        choice, traces, (((1,), (1,)), ((), ())), preferred_element_type=F32
    )
    out_ref[...] = (chosen[:, :PACKED] + chosen[:, PACKED:]).reshape(out_ref.shape)


def one_hot(source, count, base):
    row = lax.broadcasted_iota(jnp.int32, (count, source.shape[1]), 0) + base
    return jnp.where(row == source, 1.0, 0.0).astype(BF16)


def row_of_faces(ref, lead=()):
    return jnp.concatenate([ref[lead + (slice(f, f + 1),)] for f in range(4)], axis=1)


def flux_h(traces, n, half):
    j = [traces[c * PADDED : (c + 1) * PADDED] for c in range(6)]
    along = n[0] * j[0] + n[1] * j[1] + n[2] * j[2]
    parts = [
        (-(n[1] * j[5] - n[2] * j[4]) + j[0] - along * n[0]) * half,
        (-(n[2] * j[3] - n[0] * j[5]) + j[1] - along * n[1]) * half,
        (-(n[0] * j[4] - n[1] * j[3]) + j[2] - along * n[2]) * half,
    ]
    return jnp.concatenate(parts, axis=0)


def turned(flux, permutation, turn):
    variants = mm(turn, stacked_values(flux))
    out = variants[:HALF]
    for p in range(1, 6):
        out = jnp.where(permutation == p, variants[p * HALF : (p + 1) * HALF], out)
    return out


def lifted_from(flux, n, lift):
    h = [flux[c * PADDED : (c + 1) * PADDED] for c in range(3)]
    e = [n[(c + 1) % 3] * h[(c + 2) % 3] - n[(c + 2) % 3] * h[(c + 1) % 3] for c in range(3)]
    elements = flux.shape[1] // 4
    out = []
    for x in h + e:
        x = jnp.concatenate([x[:, f * elements : (f + 1) * elements] for f in range(4)], axis=0)
        out.append(split_product(lift, stacked_values(x)))
    return out


def normals(geom_ref):
    n = [row_of_faces(geom_ref, (k,)) for k in range(4)]
    return n[:3], 0.5 * n[3]


def alive(live_ref, elements):
    return (lax.broadcasted_iota(jnp.int32, (1, elements), 1) < live_ref[0]).astype(F32)


def first_kernel(
    live_ref,
    fields_hbm,
    send_hbm,
    pick_hbm,
    out_ref,
    state_ref,
    traces_ref,
    choice_ref,
    fields_ref,
    send_ref,
    pick_ref,
    sems,
):
    elements = fields_ref.shape[2]
    send_copy = pltpu.make_async_copy(send_hbm, send_ref, sems.at[0])
    fields_copy = pltpu.make_async_copy(fields_hbm, fields_ref, sems.at[1])
    pick_copy = pltpu.make_async_copy(pick_hbm, pick_ref, sems.at[2])
    send_copy.start()
    fields_copy.start()
    pick_copy.start()
    send_copy.wait()
    choice_ref[...] = outgoing_choice(send_ref[...], 4 * elements)
    fields_copy.wait()
    state = fields_ref[...].reshape(6 * NODES, elements) * alive(live_ref, elements)
    state_ref[...] = state.reshape(state_ref.shape)
    pick_copy.wait()
    traces = traces_of(state, pick_ref[...])
    traces_ref[...] = traces
    pack(choice_ref[...], traces, out_ref)


def local_kernel(
    live_ref,
    state_ref,
    traces_ref,
    metric_ref,
    geom_ref,
    source_ref,
    permutation_ref,
    derivatives_ref,
    lift_ref,
    pad_ref,
    turn_ref,
    spread_lift_ref,
    spread_node_ref,
    swapped_ref,
    out_ref,
):
    elements = state_ref.shape[2]
    slots = swapped_ref.shape[1] // 3
    own = high_over_low(swapped_ref[:, slots : 2 * slots].reshape(-1, PACKED))
    own_base = 4 * elements + own.shape[1]
    n, half = normals(geom_ref)
    source, permutation = row_of_faces(source_ref), row_of_faces(permutation_ref)
    lift = stacked_weights(lift_ref[...], spread_lift_ref)
    traces = traces_ref[...]
    gathered = []
    for f in range(4):
        source_row = source_ref[f : f + 1]
        near = mm(traces, one_hot(source_row, 4 * elements, 0))
        far = mm(own, one_hot(source_row, own.shape[1], own_base))
        gathered.append((near + far).astype(BF16))
    gathered = jnp.concatenate(gathered, axis=1)
    flux = turned(flux_h(mm(pad_ref[...], gathered), n, half), permutation, turn_ref[...])
    flux = flux - flux_h(mm(pad_ref[...], traces), n, half)
    rate = lifted_from(flux, n, lift)
    nabla = stacked_weights(derivatives_ref[...].reshape(3 * NODES, NODES), spread_node_ref)
    for c in range(6):
        slopes = split_product(nabla, stacked_values(state_ref[c]))
        s0, s1, s2 = (slopes[m * NODES : (m + 1) * NODES] for m in range(3))

        def gradient(x):
            return (
                metric_ref[x : x + 1] * s0
                + metric_ref[3 + x : 4 + x] * s1
                + metric_ref[6 + x : 7 + x] * s2
            )

        first, second = (c + 1) % 3, (c + 2) % 3
        base = 0 if c >= 3 else 3
        sign = -1.0 if c >= 3 else 1.0
        rate[base + first] = rate[base + first] + sign * gradient(second)
        rate[base + second] = rate[base + second] - sign * gradient(first)
    for c in range(6):
        out_ref[c] = rate[c]


def partner_choice(source, slots):
    even = even_group()
    near = source.shape[1]
    far = near + 2 * slots
    bases = [jnp.where(even, near, far), jnp.where(even, far, near)]
    return jnp.concatenate([one_hot(source, slots, base) for base in bases], axis=0)


def high_over_low(table):
    high, low = halves(jnp.transpose(table, (1, 0)))
    return jnp.concatenate([high, low], axis=0)


def received_flux(tables, choice, geom_ref, permutation_ref, pad_ref, turn_ref):
    columns = [high_over_low(table) for table in tables]
    n, half = normals(geom_ref)
    gathered = mm(jnp.concatenate(columns, axis=1), choice).astype(BF16)
    flux = flux_h(mm(pad_ref[...], gathered), n, half)
    return turned(flux, row_of_faces(permutation_ref), turn_ref[...]), n


def split_kernel(live_ref, swapped_ref, first_ref, other_ref):
    slots = first_ref.shape[1]
    first_ref[...] = swapped_ref[:, :slots]
    other_ref[...] = swapped_ref[:, 2 * slots :]


def final_kernel(
    step,
    live_ref,
    state_ref,
    residual_ref,
    partial_ref,
    first_ref,
    other_ref,
    source_ref,
    geom_ref,
    permutation_ref,
    ratio_ref,
    curved_ref,
    lift_ref,
    pad_ref,
    turn_ref,
    spread_lift_ref,
    pick_ref,
    send_ref,
    *out_refs,
):
    tables = [r[...].reshape(-1, PACKED) for r in (first_ref, other_ref)]
    choice = partner_choice(row_of_faces(source_ref), tables[0].shape[0])
    flux, n = received_flux(tables, choice, geom_ref, permutation_ref, pad_ref, turn_ref)
    lifted = lifted_from(flux, n, stacked_weights(lift_ref[...], spread_lift_ref))
    scaling = jnp.where(curved_ref[...] == 1, ratio_ref[...], 1.0)
    scaling = scaling * alive(live_ref, scaling.shape[1])
    state_out, residual_out = out_refs[:2]
    advanced = []
    for c in range(6):
        residual = TIME_STEP * ((partial_ref[c] + lifted[c]) * scaling)
        if step > 0:
            residual = RK_A[step] * residual_ref[c] + residual
        state = state_ref[c] + RK_B[step] * residual
        state_out[c] = state
        residual_out[c] = residual
        advanced.append(state)
    if step == 0:
        traces = traces_of(jnp.concatenate(advanced, axis=0), pick_ref[...])
        out_refs[3][...] = traces
        pack(outgoing_choice(send_ref[...], traces.shape[1]), traces, out_refs[2])


VMEM = pl.BlockSpec(memory_space=pltpu.VMEM)
SMEM = pl.BlockSpec(memory_space=pltpu.SMEM)
HBM = pl.BlockSpec(memory_space=pltpu.HBM)


def call(kernel, space, count, out_shape, name, flops, scratch=()):
    return pl.pallas_call(
        kernel,
        out_shape=out_shape,
        in_specs=[SMEM] + [space] * count,
        out_specs=jax.tree.map(lambda _: VMEM, out_shape),
        scratch_shapes=scratch,
        compiler_params=pltpu.CompilerParams(vmem_limit_bytes=24 * 1024 * 1024),
        cost_estimate=pl.CostEstimate(flops=flops, bytes_accessed=4_000_000, transcendentals=0),
        name=name,
    )


def on_device(
    fields,
    metric,
    face_geom,
    jacobian_ratio,
    curved,
    derivatives,
    lift_matrix,
    live_count,
    send_list,
    face_source,
    face_permutation,
):
    elements = fields.shape[2]
    pick, pad, turn, spread_lift, spread_node = (jnp.asarray(a) for a in constant_matrices())
    slots = send_list.shape[3]
    send = send_list.reshape(24, slots)
    curved_row = curved.reshape(1, elements)
    shape = jax.ShapeDtypeStruct
    whole = shape((6, NODES, elements), F32)
    outgoing_shape = shape((8, 3 * slots, PACKED), F32)
    traces_shape = shape((2 * PACKED, 4 * elements), BF16)

    outgoing, current, traces = call(
        first_kernel,
        HBM,
        3,
        [outgoing_shape, whole, traces_shape],
        "first",
        1_000_000_000,
        scratch=[
            pltpu.VMEM((24 * slots, 4 * elements), BF16),
            pltpu.VMEM(fields.shape, F32),
            pltpu.VMEM(send.shape, jnp.int32),
            pltpu.VMEM(pick.shape, BF16),
            pltpu.SemaphoreType.DMA((3,)),
        ],
    )(live_count, *(pltpu.with_memory_space_constraint(x, pltpu.HBM) for x in (fields, send, pick)))
    residual = current
    for step in range(2):
        swapped = lax.all_to_all(outgoing, "sub", split_axis=0, concat_axis=0, tiled=True)
        first, other = call(
            split_kernel, VMEM, 1, [shape((8, slots, PACKED), F32)] * 2, "split", 1_000_000
        )(live_count, swapped)
        first = swapped_pairs(first, "dom", 0)
        other = swapped_pairs(other, "dom", 1)
        partial = call(local_kernel, VMEM, 13, whole, "local", 4_000_000_000)(
            live_count,
            current,
            traces,
            metric,
            face_geom,
            face_source,
            face_permutation,
            derivatives,
            lift_matrix,
            pad,
            turn,
            spread_lift,
            spread_node,
            swapped,
        )
        shapes = [whole, whole] + ([outgoing_shape, traces_shape] if step == 0 else [])
        current, residual, *rest = call(
            functools.partial(final_kernel, step), VMEM, 16, shapes, "final", 3_000_000_000
        )(
            live_count,
            current,
            residual,
            partial,
            first,
            other,
            face_source,
            face_geom,
            face_permutation,
            jacobian_ratio,
            curved_row,
            lift_matrix,
            pad,
            turn,
            spread_lift,
            pick,
            send,
        )
        if rest:
            outgoing, traces = rest
    return (current, residual)


def solution(mesh):
    return jax.shard_map(
        on_device,
        mesh=mesh,
        in_specs=(
            P(None, None, ("dom", "sub")),
            P(None, ("dom", "sub")),
            P(None, None, ("dom", "sub")),
            P(None, ("dom", "sub")),
            P(("dom", "sub")),
            P(),
            P(),
            P(("dom", "sub")),
            P(("dom", "sub"), None, None, None),
            P(None, ("dom", "sub")),
            P(None, ("dom", "sub")),
        ),
        out_specs=(P(None, None, ("dom", "sub")), P(None, None, ("dom", "sub"))),
        check_vma=False,
    )
```

```python
import functools

import jax
import jax.numpy as jnp
import ml_dtypes
import numpy as np
from jax import lax
from jax.experimental import pallas as pl
from jax.experimental.pallas import tpu as pltpu
from jax.sharding import PartitionSpec as P

RK_A = (0.0, -567301805773.0 / 1357537059087.0)
RK_B = (1432997174477.0 / 9575080441755.0, 5161836677717.0 / 13612068292357.0)
TIME_STEP = 0.5
SYMMETRIES = ((0, 1, 2), (1, 2, 0), (2, 0, 1), (0, 2, 1), (2, 1, 0), (1, 0, 2))

NODES = 56
TRACE = 21
PADDED = 24
TRIPLE = 64
PACKED = 2 * TRIPLE
EXT = 6 * PADDED
HALF = 3 * PADDED
F32 = jnp.float32
BF16 = jnp.bfloat16


def swapped_pairs(array, axis, first):
    count = lax.axis_size(axis)
    pairs = []
    for low in range(first, count - 1, 2):
        pairs += [(low, low + 1), (low + 1, low)]
    return lax.ppermute(array, axis, pairs)


def node_tables():
    volume_nodes = [(i, j, k) for i in range(6) for j in range(6 - i) for k in range(6 - i - j)]
    volume_index = {v: n for n, v in enumerate(volume_nodes)}
    triangle = [(a, b) for a in range(6) for b in range(6 - a)]
    triangle_index = {t: n for n, t in enumerate(triangle)}
    face_nodes = np.array(
        [
            [volume_index[a, b, 0] for a, b in triangle],
            [volume_index[a, 0, b] for a, b in triangle],
            [volume_index[a, b, 5 - a - b] for a, b in triangle],
            [volume_index[0, a, b] for a, b in triangle],
        ],
        np.int32,
    )
    permuted = np.array(
        [
            [triangle_index[(a, b, 5 - a - b)[q[0]], (a, b, 5 - a - b)[q[1]]] for a, b in triangle]
            for q in SYMMETRIES
        ],
        np.int32,
    )
    return (face_nodes, permuted)


def constant_matrices():
    face_nodes, permuted = node_tables()
    pick = np.zeros((4 * TRIPLE, 3 * NODES), np.float32)
    pad = np.zeros((EXT, 2 * PACKED), np.float32)
    turn = np.zeros((5 * HALF, 2 * HALF), np.float32)
    for m in range(TRACE):
        for c in range(6):
            for part in range(2):
                place = part * PACKED + (c // 3) * TRIPLE + (c % 3) * TRACE + m
                pad[c * PADDED + m, place] = 1
        for c in range(3):
            for f in range(4):
                pick[f * TRIPLE + c * TRACE + m, c * NODES + face_nodes[f, m]] = 1
            for p in range(1, 6):
                for part in range(2):
                    row = (p - 1) * HALF + c * PADDED
                    turn[row + m, part * HALF + c * PADDED + permuted[p, m]] = 1
    both = np.zeros((2 * EXT, 2 * PACKED), np.float32)
    both[:EXT, :PACKED] = both[EXT:, PACKED:] = pad[:, :PACKED]
    spread_lift = np.zeros((2, 4 * TRACE, 8 * PADDED), np.float32)
    for f in range(4):
        for m in range(TRACE):
            spread_lift[0, f * TRACE + m, f * PADDED + m] = 1
            spread_lift[0, f * TRACE + m, (4 + f) * PADDED + m] = 1
            spread_lift[1, f * TRACE + m, f * PADDED + m] = 1
    spread_node = np.zeros((2, NODES, 2 * NODES), np.float32)
    spread_node[0, :, :NODES] = spread_node[0, :, NODES:] = np.eye(NODES)
    spread_node[1, :, :NODES] = np.eye(NODES)
    return [a.astype(ml_dtypes.bfloat16) for a in (pick, pad, both, turn, spread_lift, spread_node)]


def mm(a, b):
    return jnp.dot(a, b, preferred_element_type=F32)


def halves(x):
    high = x.astype(BF16)
    return high, (x - high.astype(F32)).astype(BF16)


def stacked_weights(weights, spread):
    high, low = halves(weights)
    return jnp.concatenate([mm(high, spread[0]), mm(low, spread[1])], axis=0).astype(BF16)


def stacked_values(x):
    high = x.astype(BF16).astype(F32)
    return jnp.concatenate([high, x - high], axis=0).astype(BF16)


def split_product(weights, values):
    both = mm(weights, values)
    rows = both.shape[0] // 2
    return both[:rows] + both[rows:]


def traces_of(state, pick):
    parts = []
    for half in range(2):
        high, low = halves(state[half * 3 * NODES : (half + 1) * 3 * NODES])
        faces = [mm(pick, part).astype(BF16) for part in (high, low)]
        parts.append(
            [
                jnp.concatenate([x[f * TRIPLE : (f + 1) * TRIPLE] for f in range(4)], axis=1)
                for x in faces
            ]
        )
    return jnp.concatenate([parts[0][0], parts[1][0], parts[0][1], parts[1][1]], axis=0)


def even_group():
    return lax.rem(lax.axis_index("dom"), 2) == 0


def outgoing_choice(send, faces):
    even = even_group()
    low, own, high = send[:8], send[8:16], send[16:]
    ordered = [jnp.where(even, high, low), own, jnp.where(even, low, high)]
    columns = jnp.transpose(jnp.concatenate(ordered, axis=0), (1, 0))
    lane = lax.broadcasted_iota(jnp.int32, (send.shape[1], faces), 1)
    rows = []
    for j in range(8):
        for block in range(3):
            r = block * 8 + j
            rows.append(jnp.where(lane == columns[:, r : r + 1], 1.0, 0.0).astype(BF16))
    return jnp.concatenate(rows, axis=0)


def pack(choice, traces, out_ref):
    chosen = lax.dot_general(
        choice, traces, (((1,), (1,)), ((), ())), preferred_element_type=F32
    )
    out_ref[...] = (chosen[:, :PACKED] + chosen[:, PACKED:]).reshape(out_ref.shape)


def one_hot(source, count, base):
    row = lax.broadcasted_iota(jnp.int32, (count, source.shape[1]), 0) + base
    return jnp.where(row == source, 1.0, 0.0).astype(BF16)


def row_of_faces(ref, lead=()):
    return jnp.concatenate([ref[lead + (slice(f, f + 1),)] for f in range(4)], axis=1)


def flux_h(traces, n, half):
    j = [traces[c * PADDED : (c + 1) * PADDED] for c in range(6)]
    along = n[0] * j[0] + n[1] * j[1] + n[2] * j[2]
    parts = [
        (-(n[1] * j[5] - n[2] * j[4]) + j[0] - along * n[0]) * half,
        (-(n[2] * j[3] - n[0] * j[5]) + j[1] - along * n[1]) * half,
        (-(n[0] * j[4] - n[1] * j[3]) + j[2] - along * n[2]) * half,
    ]
    return jnp.concatenate(parts, axis=0)


def turned(flux, permutation, turn):
    variants = mm(turn, stacked_values(flux))
    out = flux
    for p in range(1, 6):
        out = jnp.where(permutation == p, variants[(p - 1) * HALF : p * HALF], out)
    return out


def lifted_from(flux, n, lift):
    h = [flux[c * PADDED : (c + 1) * PADDED] for c in range(3)]
    e = [n[(c + 1) % 3] * h[(c + 2) % 3] - n[(c + 2) % 3] * h[(c + 1) % 3] for c in range(3)]
    elements = flux.shape[1] // 4
    out = []
    for x in h + e:
        x = jnp.concatenate([x[:, f * elements : (f + 1) * elements] for f in range(4)], axis=0)
        out.append(split_product(lift, stacked_values(x)))
    return out


def normals(geom_ref):
    n = [row_of_faces(geom_ref, (k,)) for k in range(4)]
    return n[:3], 0.5 * n[3]


def alive(live_ref, elements):
    return (lax.broadcasted_iota(jnp.int32, (1, elements), 1) < live_ref[0]).astype(F32)


def first_kernel(
    live_ref,
    fields_hbm,
    send_hbm,
    pick_hbm,
    out_ref,
    state_ref,
    traces_ref,
    choice_ref,
    fields_ref,
    send_ref,
    pick_ref,
    sems,
):
    elements = fields_ref.shape[2]
    send_copy = pltpu.make_async_copy(send_hbm, send_ref, sems.at[0])
    fields_copy = pltpu.make_async_copy(fields_hbm, fields_ref, sems.at[1])
    pick_copy = pltpu.make_async_copy(pick_hbm, pick_ref, sems.at[2])
    send_copy.start()
    fields_copy.start()
    pick_copy.start()
    send_copy.wait()
    choice_ref[...] = outgoing_choice(send_ref[...], 4 * elements)
    fields_copy.wait()
    state = fields_ref[...].reshape(6 * NODES, elements) * alive(live_ref, elements)
    state_ref[...] = state.reshape(state_ref.shape)
    pick_copy.wait()
    traces = traces_of(state, pick_ref[...])
    traces_ref[...] = traces
    pack(choice_ref[...], traces, out_ref)


def local_kernel(
    live_ref,
    state_ref,
    traces_ref,
    metric_ref,
    geom_ref,
    source_ref,
    permutation_ref,
    derivatives_ref,
    lift_ref,
    pad_ref,
    turn_ref,
    spread_lift_ref,
    spread_node_ref,
    swapped_ref,
    out_ref,
):
    elements = state_ref.shape[2]
    slots = swapped_ref.shape[1] // 3
    own = high_over_low(swapped_ref[:, slots : 2 * slots].reshape(-1, PACKED))
    own_base = 4 * elements + own.shape[1]
    n, half = normals(geom_ref)
    source, permutation = row_of_faces(source_ref), row_of_faces(permutation_ref)
    lift = stacked_weights(lift_ref[...], spread_lift_ref)
    traces = traces_ref[...]
    gathered = []
    for f in range(4):
        source_row = source_ref[f : f + 1]
        near = mm(traces, one_hot(source_row, 4 * elements, 0))
        far = mm(own, one_hot(source_row, own.shape[1], own_base))
        gathered.append((near + far).astype(BF16))
    gathered = jnp.concatenate(gathered, axis=1)
    flux = turned(flux_h(mm(pad_ref[...], gathered), n, half), permutation, turn_ref[...])
    flux = flux - flux_h(mm(pad_ref[...], traces), n, half)
    rate = lifted_from(flux, n, lift)
    nabla = stacked_weights(derivatives_ref[...].reshape(3 * NODES, NODES), spread_node_ref)
    for c in range(6):
        slopes = split_product(nabla, stacked_values(state_ref[c]))
        s0, s1, s2 = (slopes[m * NODES : (m + 1) * NODES] for m in range(3))

        def gradient(x):
            return (
                metric_ref[x : x + 1] * s0
                + metric_ref[3 + x : 4 + x] * s1
                + metric_ref[6 + x : 7 + x] * s2
            )

        first, second = (c + 1) % 3, (c + 2) % 3
        base = 0 if c >= 3 else 3
        sign = -1.0 if c >= 3 else 1.0
        rate[base + first] = rate[base + first] + sign * gradient(second)
        rate[base + second] = rate[base + second] - sign * gradient(first)
    for c in range(6):
        out_ref[c] = rate[c]


def partner_choice(source, slots):
    even = even_group()
    near = source.shape[1]
    far = near + 2 * slots
    bases = [jnp.where(even, near, far), jnp.where(even, far, near)]
    return jnp.concatenate([one_hot(source, slots, base) for base in bases], axis=0)


def high_over_low(table):
    high, low = halves(jnp.transpose(table, (1, 0)))
    return jnp.concatenate([high, low], axis=0)


def received_flux(tables, choice, geom_ref, permutation_ref, both_ref, turn_ref):
    columns = [high_over_low(table) for table in tables]
    n, half = normals(geom_ref)
    table = mm(both_ref[...], jnp.concatenate(columns, axis=1)).astype(BF16)
    flux = flux_h(split_product(table, choice), n, half)
    return turned(flux, row_of_faces(permutation_ref), turn_ref[...]), n


def split_kernel(live_ref, swapped_ref, other_ref, first_ref):
    slots = first_ref.shape[1]
    first_ref[...] = swapped_ref[:, :slots]
    other_ref[...] = swapped_ref[:, 2 * slots :]


def final_kernel(
    step,
    live_ref,
    state_ref,
    residual_ref,
    partial_ref,
    other_ref,
    first_ref,
    source_ref,
    geom_ref,
    permutation_ref,
    ratio_ref,
    curved_ref,
    lift_ref,
    both_ref,
    turn_ref,
    spread_lift_ref,
    pick_ref,
    send_ref,
    *out_refs,
):
    tables = [r[...].reshape(-1, PACKED) for r in (first_ref, other_ref)]
    choice = partner_choice(row_of_faces(source_ref), tables[0].shape[0])
    flux, n = received_flux(tables, choice, geom_ref, permutation_ref, both_ref, turn_ref)
    lifted = lifted_from(flux, n, stacked_weights(lift_ref[...], spread_lift_ref))
    scaling = jnp.where(curved_ref[...] == 1, ratio_ref[...], 1.0)
    scaling = scaling * alive(live_ref, scaling.shape[1])
    state_out, residual_out = out_refs[:2]
    advanced = []
    for c in range(6):
        residual = TIME_STEP * ((partial_ref[c] + lifted[c]) * scaling)
        if step > 0:
            residual = RK_A[step] * residual_ref[c] + residual
        state = state_ref[c] + RK_B[step] * residual
        state_out[c] = state
        residual_out[c] = residual
        advanced.append(state)
    if step == 0:
        traces = traces_of(jnp.concatenate(advanced, axis=0), pick_ref[...])
        out_refs[3][...] = traces
        pack(outgoing_choice(send_ref[...], traces.shape[1]), traces, out_refs[2])


VMEM = pl.BlockSpec(memory_space=pltpu.VMEM)
SMEM = pl.BlockSpec(memory_space=pltpu.SMEM)
HBM = pl.BlockSpec(memory_space=pltpu.HBM)


def call(kernel, space, count, out_shape, name, flops, scratch=()):
    return pl.pallas_call(
        kernel,
        out_shape=out_shape,
        in_specs=[SMEM] + [space] * count,
        out_specs=jax.tree.map(lambda _: VMEM, out_shape),
        scratch_shapes=scratch,
        compiler_params=pltpu.CompilerParams(vmem_limit_bytes=24 * 1024 * 1024),
        cost_estimate=pl.CostEstimate(flops=flops, bytes_accessed=4_000_000, transcendentals=0),
        name=name,
    )


def on_device(
    fields,
    metric,
    face_geom,
    jacobian_ratio,
    curved,
    derivatives,
    lift_matrix,
    live_count,
    send_list,
    face_source,
    face_permutation,
):
    elements = fields.shape[2]
    pick, pad, both, turn, spread_lift, spread_node = (jnp.asarray(a) for a in constant_matrices())
    slots = send_list.shape[3]
    send = send_list.reshape(24, slots)
    curved_row = curved.reshape(1, elements)
    shape = jax.ShapeDtypeStruct
    whole = shape((6, NODES, elements), F32)
    outgoing_shape = shape((8, 3 * slots, PACKED), F32)
    traces_shape = shape((2 * PACKED, 4 * elements), BF16)

    outgoing, current, traces = call(
        first_kernel,
        HBM,
        3,
        [outgoing_shape, whole, traces_shape],
        "first",
        1_000_000_000,
        scratch=[
            pltpu.VMEM((24 * slots, 4 * elements), BF16),
            pltpu.VMEM(fields.shape, F32),
            pltpu.VMEM(send.shape, jnp.int32),
            pltpu.VMEM(pick.shape, BF16),
            pltpu.SemaphoreType.DMA((3,)),
        ],
    )(live_count, *(pltpu.with_memory_space_constraint(x, pltpu.HBM) for x in (fields, send, pick)))
    residual = current
    for step in range(2):
        swapped = lax.all_to_all(outgoing, "sub", split_axis=0, concat_axis=0, tiled=True)
        other, first = call(
            split_kernel, VMEM, 1, [shape((8, slots, PACKED), F32)] * 2, "split", 1_000_000
        )(live_count, swapped)
        other = swapped_pairs(other, "dom", 1)
        first = swapped_pairs(first, "dom", 0)
        partial = call(local_kernel, VMEM, 13, whole, "local", 4_000_000_000)(
            live_count,
            current,
            traces,
            metric,
            face_geom,
            face_source,
            face_permutation,
            derivatives,
            lift_matrix,
            pad,
            turn,
            spread_lift,
            spread_node,
            swapped,
        )
        shapes = [whole, whole] + ([outgoing_shape, traces_shape] if step == 0 else [])
        current, residual, *rest = call(
            functools.partial(final_kernel, step), VMEM, 16, shapes, "final", 3_000_000_000
        )(
            live_count,
            current,
            residual,
            partial,
            other,
            first,
            face_source,
            face_geom,
            face_permutation,
            jacobian_ratio,
            curved_row,
            lift_matrix,
            both,
            turn,
            spread_lift,
            pick,
            send,
        )
        if rest:
            outgoing, traces = rest
    return (current, residual)


def solution(mesh):
    return jax.shard_map(
        on_device,
        mesh=mesh,
        in_specs=(
            P(None, None, ("dom", "sub")),
            P(None, ("dom", "sub")),
            P(None, None, ("dom", "sub")),
            P(None, ("dom", "sub")),
            P(("dom", "sub")),
            P(),
            P(),
            P(("dom", "sub")),
            P(("dom", "sub"), None, None, None),
            P(None, ("dom", "sub")),
            P(None, ("dom", "sub")),
        ),
        out_specs=(P(None, None, ("dom", "sub")), P(None, None, ("dom", "sub"))),
        check_vma=False,
    )
```

```python
import functools

import jax
import jax.numpy as jnp
import ml_dtypes
import numpy as np
from jax import lax
from jax.experimental import pallas as pl
from jax.experimental.pallas import tpu as pltpu
from jax.sharding import PartitionSpec as P

RK_A = (0.0, -567301805773.0 / 1357537059087.0)
RK_B = (1432997174477.0 / 9575080441755.0, 5161836677717.0 / 13612068292357.0)
TIME_STEP = 0.5
SYMMETRIES = ((0, 1, 2), (1, 2, 0), (2, 0, 1), (0, 2, 1), (2, 1, 0), (1, 0, 2))

NODES = 56
TRACE = 21
PADDED = 24
TRIPLE = 64
PACKED = 2 * TRIPLE
EXT = 6 * PADDED
HALF = 3 * PADDED
F32 = jnp.float32
BF16 = jnp.bfloat16


def swapped_pairs(array, axis, first):
    count = lax.axis_size(axis)
    pairs = []
    for low in range(first, count - 1, 2):
        pairs += [(low, low + 1), (low + 1, low)]
    return lax.ppermute(array, axis, pairs)


def node_tables():
    volume_nodes = [(i, j, k) for i in range(6) for j in range(6 - i) for k in range(6 - i - j)]
    volume_index = {v: n for n, v in enumerate(volume_nodes)}
    triangle = [(a, b) for a in range(6) for b in range(6 - a)]
    triangle_index = {t: n for n, t in enumerate(triangle)}
    face_nodes = np.array(
        [
            [volume_index[a, b, 0] for a, b in triangle],
            [volume_index[a, 0, b] for a, b in triangle],
            [volume_index[a, b, 5 - a - b] for a, b in triangle],
            [volume_index[0, a, b] for a, b in triangle],
        ],
        np.int32,
    )
    permuted = np.array(
        [
            [triangle_index[(a, b, 5 - a - b)[q[0]], (a, b, 5 - a - b)[q[1]]] for a, b in triangle]
            for q in SYMMETRIES
        ],
        np.int32,
    )
    return (face_nodes, permuted)


def constant_matrices():
    face_nodes, permuted = node_tables()
    pick = np.zeros((4 * TRIPLE, 3 * NODES), np.float32)
    pad = np.zeros((EXT, 2 * PACKED), np.float32)
    turn = np.zeros((5 * HALF, 2 * HALF), np.float32)
    for m in range(TRACE):
        for c in range(6):
            for part in range(2):
                place = part * PACKED + (c // 3) * TRIPLE + (c % 3) * TRACE + m
                pad[c * PADDED + m, place] = 1
        for c in range(3):
            for f in range(4):
                pick[f * TRIPLE + c * TRACE + m, c * NODES + face_nodes[f, m]] = 1
            for p in range(1, 6):
                for part in range(2):
                    row = (p - 1) * HALF + c * PADDED
                    turn[row + m, part * HALF + c * PADDED + permuted[p, m]] = 1
    both = np.zeros((2 * EXT, 2 * PACKED), np.float32)
    both[:EXT, :PACKED] = both[EXT:, PACKED:] = pad[:, :PACKED]
    spread_lift = np.zeros((2, 4 * TRACE, 8 * PADDED), np.float32)
    for f in range(4):
        for m in range(TRACE):
            spread_lift[0, f * TRACE + m, f * PADDED + m] = 1
            spread_lift[0, f * TRACE + m, (4 + f) * PADDED + m] = 1
            spread_lift[1, f * TRACE + m, f * PADDED + m] = 1
    spread_node = np.zeros((2, NODES, 2 * NODES), np.float32)
    spread_node[0, :, :NODES] = spread_node[0, :, NODES:] = np.eye(NODES)
    spread_node[1, :, :NODES] = np.eye(NODES)
    return [a.astype(ml_dtypes.bfloat16) for a in (pick, pad, both, turn, spread_lift, spread_node)]


def mm(a, b):
    return jnp.dot(a, b, preferred_element_type=F32)


def halves(x):
    high = x.astype(BF16)
    return high, (x - high.astype(F32)).astype(BF16)


def stacked_weights(weights, spread):
    high, low = halves(weights)
    return jnp.concatenate([mm(high, spread[0]), mm(low, spread[1])], axis=0).astype(BF16)


def stacked_values(x):
    high = x.astype(BF16).astype(F32)
    return jnp.concatenate([high, x - high], axis=0).astype(BF16)


def split_product(weights, values):
    both = mm(weights, values)
    rows = both.shape[0] // 2
    return both[:rows] + both[rows:]


def traces_of(state, pick):
    parts = []
    for half in range(2):
        high, low = halves(state[half * 3 * NODES : (half + 1) * 3 * NODES])
        faces = [mm(pick, part).astype(BF16) for part in (high, low)]
        parts.append(
            [
                jnp.concatenate([x[f * TRIPLE : (f + 1) * TRIPLE] for f in range(4)], axis=1)
                for x in faces
            ]
        )
    return jnp.concatenate([parts[0][0], parts[1][0], parts[0][1], parts[1][1]], axis=0)


def even_group():
    return lax.rem(lax.axis_index("dom"), 2) == 0


def outgoing_choice(send, faces):
    even = even_group()
    low, own, high = send[:8], send[8:16], send[16:]
    ordered = [jnp.where(even, high, low), own, jnp.where(even, low, high)]
    columns = jnp.transpose(jnp.concatenate(ordered, axis=0), (1, 0))
    lane = lax.broadcasted_iota(jnp.int32, (send.shape[1], faces), 1)
    rows = []
    for j in range(8):
        for block in range(3):
            r = block * 8 + j
            rows.append(jnp.where(lane == columns[:, r : r + 1], 1.0, 0.0).astype(BF16))
    return jnp.concatenate(rows, axis=0)


def pack(choice, traces, out_ref):
    chosen = lax.dot_general(
        choice, traces, (((1,), (1,)), ((), ())), preferred_element_type=F32
    )
    out_ref[...] = (chosen[:, :PACKED] + chosen[:, PACKED:]).reshape(out_ref.shape)


def one_hot(source, count, base):
    row = lax.broadcasted_iota(jnp.int32, (count, source.shape[1]), 0) + base
    return jnp.where(row == source, 1.0, 0.0).astype(BF16)


def row_of_faces(ref, lead=()):
    return jnp.concatenate([ref[lead + (slice(f, f + 1),)] for f in range(4)], axis=1)


def flux_h(traces, n, half):
    j = [traces[c * PADDED : (c + 1) * PADDED] for c in range(6)]
    along = n[0] * j[0] + n[1] * j[1] + n[2] * j[2]
    parts = [
        (-(n[1] * j[5] - n[2] * j[4]) + j[0] - along * n[0]) * half,
        (-(n[2] * j[3] - n[0] * j[5]) + j[1] - along * n[1]) * half,
        (-(n[0] * j[4] - n[1] * j[3]) + j[2] - along * n[2]) * half,
    ]
    return jnp.concatenate(parts, axis=0)


def turned(flux, permutation, turn):
    variants = mm(turn, stacked_values(flux))
    out = flux
    for p in range(1, 6):
        out = jnp.where(permutation == p, variants[(p - 1) * HALF : p * HALF], out)
    return out


def lifted_from(flux, n, lift):
    h = [flux[c * PADDED : (c + 1) * PADDED] for c in range(3)]
    e = [n[(c + 1) % 3] * h[(c + 2) % 3] - n[(c + 2) % 3] * h[(c + 1) % 3] for c in range(3)]
    elements = flux.shape[1] // 4
    out = []
    for x in h + e:
        x = jnp.concatenate([x[:, f * elements : (f + 1) * elements] for f in range(4)], axis=0)
        out.append(split_product(lift, stacked_values(x)))
    return out


def normals(geom_ref):
    n = [row_of_faces(geom_ref, (k,)) for k in range(4)]
    return n[:3], 0.5 * n[3]


def alive(live_ref, elements):
    return (lax.broadcasted_iota(jnp.int32, (1, elements), 1) < live_ref[0]).astype(F32)


def first_kernel(
    live_ref,
    fields_hbm,
    send_hbm,
    pick_hbm,
    out_ref,
    state_ref,
    traces_ref,
    choice_ref,
    fields_ref,
    send_ref,
    pick_ref,
    sems,
):
    elements = fields_ref.shape[2]
    send_copy = pltpu.make_async_copy(send_hbm, send_ref, sems.at[0])
    fields_copy = pltpu.make_async_copy(fields_hbm, fields_ref, sems.at[1])
    pick_copy = pltpu.make_async_copy(pick_hbm, pick_ref, sems.at[2])
    send_copy.start()
    fields_copy.start()
    pick_copy.start()
    send_copy.wait()
    choice_ref[...] = outgoing_choice(send_ref[...], 4 * elements)
    fields_copy.wait()
    state = fields_ref[...].reshape(6 * NODES, elements) * alive(live_ref, elements)
    state_ref[...] = state.reshape(state_ref.shape)
    pick_copy.wait()
    traces = traces_of(state, pick_ref[...])
    traces_ref[...] = traces
    pack(choice_ref[...], traces, out_ref)


def local_kernel(
    live_ref,
    state_ref,
    traces_ref,
    metric_ref,
    geom_ref,
    source_ref,
    permutation_ref,
    derivatives_ref,
    lift_ref,
    pad_ref,
    turn_ref,
    spread_lift_ref,
    spread_node_ref,
    swapped_ref,
    out_ref,
):
    elements = state_ref.shape[2]
    slots = swapped_ref.shape[1] // 3
    own = high_over_low(swapped_ref[:, slots : 2 * slots].reshape(-1, PACKED))
    own_base = 4 * elements + own.shape[1]
    n, half = normals(geom_ref)
    source, permutation = row_of_faces(source_ref), row_of_faces(permutation_ref)
    lift = stacked_weights(lift_ref[...], spread_lift_ref)
    traces = traces_ref[...]
    gathered = []
    for f in range(4):
        source_row = source_ref[f : f + 1]
        near = mm(traces, one_hot(source_row, 4 * elements, 0))
        far = mm(own, one_hot(source_row, own.shape[1], own_base))
        gathered.append((near + far).astype(BF16))
    gathered = jnp.concatenate(gathered, axis=1)
    flux = turned(flux_h(mm(pad_ref[...], gathered), n, half), permutation, turn_ref[...])
    flux = flux - flux_h(mm(pad_ref[...], traces), n, half)
    rate = lifted_from(flux, n, lift)
    nabla = stacked_weights(derivatives_ref[...].reshape(3 * NODES, NODES), spread_node_ref)
    for c in range(6):
        slopes = split_product(nabla, stacked_values(state_ref[c]))
        s0, s1, s2 = (slopes[m * NODES : (m + 1) * NODES] for m in range(3))

        def gradient(x):
            return (
                metric_ref[x : x + 1] * s0
                + metric_ref[3 + x : 4 + x] * s1
                + metric_ref[6 + x : 7 + x] * s2
            )

        first, second = (c + 1) % 3, (c + 2) % 3
        base = 0 if c >= 3 else 3
        sign = -1.0 if c >= 3 else 1.0
        rate[base + first] = rate[base + first] + sign * gradient(second)
        rate[base + second] = rate[base + second] - sign * gradient(first)
    for c in range(6):
        out_ref[c] = rate[c]


def partner_gather(table, is_first, source_ref, both_ref):
    source = row_of_faces(source_ref)
    count = table.shape[0]
    near, far = source.shape[1], source.shape[1] + 2 * count
    base = jnp.where(even_group() == is_first, near, far)
    padded = mm(both_ref[...], high_over_low(table)).astype(BF16)
    return split_product(padded, one_hot(source, count, base))


def early_kernel(live_ref, other_ref, source_ref, both_ref, out_ref):
    table = other_ref[...].reshape(-1, PACKED)
    out_ref[...] = partner_gather(table, False, source_ref, both_ref)


def high_over_low(table):
    high, low = halves(jnp.transpose(table, (1, 0)))
    return jnp.concatenate([high, low], axis=0)


def split_kernel(live_ref, swapped_ref, other_ref, first_ref):
    slots = first_ref.shape[1]
    first_ref[...] = swapped_ref[:, :slots]
    other_ref[...] = swapped_ref[:, 2 * slots :]


def final_kernel(
    step,
    live_ref,
    state_ref,
    residual_ref,
    partial_ref,
    early_ref,
    first_ref,
    source_ref,
    geom_ref,
    permutation_ref,
    ratio_ref,
    curved_ref,
    lift_ref,
    both_ref,
    turn_ref,
    spread_lift_ref,
    pick_ref,
    send_ref,
    *out_refs,
):
    n, half = normals(geom_ref)
    exterior = early_ref[...] + partner_gather(
        first_ref[...].reshape(-1, PACKED), True, source_ref, both_ref
    )
    flux = turned(flux_h(exterior, n, half), row_of_faces(permutation_ref), turn_ref[...])
    lifted = lifted_from(flux, n, stacked_weights(lift_ref[...], spread_lift_ref))
    scaling = jnp.where(curved_ref[...] == 1, ratio_ref[...], 1.0)
    scaling = scaling * alive(live_ref, scaling.shape[1])
    state_out, residual_out = out_refs[:2]
    advanced = []
    for c in range(6):
        residual = TIME_STEP * ((partial_ref[c] + lifted[c]) * scaling)
        if step > 0:
            residual = RK_A[step] * residual_ref[c] + residual
        state = state_ref[c] + RK_B[step] * residual
        state_out[c] = state
        residual_out[c] = residual
        advanced.append(state)
    if step == 0:
        traces = traces_of(jnp.concatenate(advanced, axis=0), pick_ref[...])
        out_refs[3][...] = traces
        pack(outgoing_choice(send_ref[...], traces.shape[1]), traces, out_refs[2])


VMEM = pl.BlockSpec(memory_space=pltpu.VMEM)
SMEM = pl.BlockSpec(memory_space=pltpu.SMEM)
HBM = pl.BlockSpec(memory_space=pltpu.HBM)


def call(kernel, space, count, out_shape, name, flops, scratch=()):
    return pl.pallas_call(
        kernel,
        out_shape=out_shape,
        in_specs=[SMEM] + [space] * count,
        out_specs=jax.tree.map(lambda _: VMEM, out_shape),
        scratch_shapes=scratch,
        compiler_params=pltpu.CompilerParams(vmem_limit_bytes=24 * 1024 * 1024),
        cost_estimate=pl.CostEstimate(flops=flops, bytes_accessed=4_000_000, transcendentals=0),
        name=name,
    )


def on_device(
    fields,
    metric,
    face_geom,
    jacobian_ratio,
    curved,
    derivatives,
    lift_matrix,
    live_count,
    send_list,
    face_source,
    face_permutation,
):
    elements = fields.shape[2]
    pick, pad, both, turn, spread_lift, spread_node = (jnp.asarray(a) for a in constant_matrices())
    slots = send_list.shape[3]
    send = send_list.reshape(24, slots)
    curved_row = curved.reshape(1, elements)
    shape = jax.ShapeDtypeStruct
    whole = shape((6, NODES, elements), F32)
    outgoing_shape = shape((8, 3 * slots, PACKED), F32)
    traces_shape = shape((2 * PACKED, 4 * elements), BF16)

    outgoing, current, traces = call(
        first_kernel,
        HBM,
        3,
        [outgoing_shape, whole, traces_shape],
        "first",
        1_000_000_000,
        scratch=[
            pltpu.VMEM((24 * slots, 4 * elements), BF16),
            pltpu.VMEM(fields.shape, F32),
            pltpu.VMEM(send.shape, jnp.int32),
            pltpu.VMEM(pick.shape, BF16),
            pltpu.SemaphoreType.DMA((3,)),
        ],
    )(live_count, *(pltpu.with_memory_space_constraint(x, pltpu.HBM) for x in (fields, send, pick)))
    residual = current
    for step in range(2):
        swapped = lax.all_to_all(outgoing, "sub", split_axis=0, concat_axis=0, tiled=True)
        other, first = call(
            split_kernel, VMEM, 1, [shape((8, slots, PACKED), F32)] * 2, "split", 1_000_000
        )(live_count, swapped)
        other = swapped_pairs(other, "dom", 1)
        first = swapped_pairs(first, "dom", 0)
        partial = call(local_kernel, VMEM, 13, whole, "local", 4_000_000_000)(
            live_count,
            current,
            traces,
            metric,
            face_geom,
            face_source,
            face_permutation,
            derivatives,
            lift_matrix,
            pad,
            turn,
            spread_lift,
            spread_node,
            swapped,
        )
        early = call(
            early_kernel, VMEM, 3, shape((EXT, 4 * elements), F32), "early", 1_000_000_000
        )(live_count, other, face_source, both)
        shapes = [whole, whole] + ([outgoing_shape, traces_shape] if step == 0 else [])
        current, residual, *rest = call(
            functools.partial(final_kernel, step), VMEM, 16, shapes, "final", 3_000_000_000
        )(
            live_count,
            current,
            residual,
            partial,
            early,
            first,
            face_source,
            face_geom,
            face_permutation,
            jacobian_ratio,
            curved_row,
            lift_matrix,
            both,
            turn,
            spread_lift,
            pick,
            send,
        )
        if rest:
            outgoing, traces = rest
    return (current, residual)


def solution(mesh):
    return jax.shard_map(
        on_device,
        mesh=mesh,
        in_specs=(
            P(None, None, ("dom", "sub")),
            P(None, ("dom", "sub")),
            P(None, None, ("dom", "sub")),
            P(None, ("dom", "sub")),
            P(("dom", "sub")),
            P(),
            P(),
            P(("dom", "sub")),
            P(("dom", "sub"), None, None, None),
            P(None, ("dom", "sub")),
            P(None, ("dom", "sub")),
        ),
        out_specs=(P(None, None, ("dom", "sub")), P(None, None, ("dom", "sub"))),
        check_vma=False,
    )
```
